128 devices in a mesh: row: 4 (over y), col: 32 (over z, x, core).
Axes of the slice: x: 4, y: 4, z: 4, core: 2. Of those that a mesh axis runs over, the one named last changes fastest.
Arguments:
- tokens: bfloat16 [768, 8192], P('col', 'row'), may hold values from -6 to 6
- gate_weight: bfloat16 [8192, 28672], P('row', 'col'), may hold values from -0.0625 to 0.0625
- up_weight: bfloat16 [8192, 28672], P('row', 'col'), may hold values from -0.0625 to 0.0625
- down_weight: bfloat16 [28672, 8192], P('col', 'row'), may hold values from -0.03125 to 0.03125
- mask_gate: int32 [128, 448], P('row', 'col'), may hold values from 0 to 1, as said below
- mask_up: int32 [128, 448], P('row', 'col'), may hold values from 0 to 1, as said below
- mask_down: int32 [448, 128], P('col', 'row'), may hold values from 0 to 1, as said below
- cotangent: bfloat16 [768, 8192], P('col', 'row'), may hold values from -1.5 to 1.5
Outputs:
- output: bfloat16 [768, 8192], P('col', 'row')
- grad_input: bfloat16 [768, 8192], P('col', 'row')
- grad_gate: bfloat16 [8192, 28672], P('row', 'col')
- grad_up: bfloat16 [8192, 28672], P('row', 'col')
- grad_down: bfloat16 [28672, 8192], P('col', 'row')
The draws below stay inside these ranges and needn't reach their ends.
Inputs may be any that keep to these rules, and one draw needn't show every extreme that they name: `mask_gate`: 1 where a 64 x 64 block of the weight is kept, 0 where it is pruned. `mask_up`: 1 where a 64 x 64 block of the weight is kept, 0 where it is pruned. `mask_down`: 1 where a 64 x 64 block of the weight is kept, 0 where it is pruned.
All inputs are finite; a program needn't handle non-finite values.
Results may differ from the reference program's by a relative error of at most 0.006.
Values may be sent and summed in bfloat16 or wider, within the bound.
No kernel may reach another device: no remote copies, remote signals or barrier semaphores. Data moves between devices by JAX's collectives and lax.ppermute only.
A program may use at most 128 MiB of HBM per device.

```python
import jax
import jax.numpy as jnp
from jax import lax

D = 8192
FF = 28672
BLOCK = 64
TOKENS = 768
DB = 128
FB = 448
N_COL = 32


def column_mask(key, salt, rows, cols, group_axis):
    base = jax.random.fold_in(key, salt)
    dens_key = jax.random.fold_in(base, 1)
    cell_key = jax.random.fold_in(base, 2)
    density = jax.random.randint(dens_key, (N_COL,), 3, 10)
    cells = jax.random.randint(cell_key, (rows, cols), 0, 10)
    if group_axis == 1:
        groups = jnp.arange(cols, dtype=jnp.int32) // (cols // N_COL)
        level = density[groups][None, :]
    else:
        groups = jnp.arange(rows, dtype=jnp.int32) // (rows // N_COL)
        level = density[groups][:, None]
    return (cells < level).astype(jnp.int32)


def draw_mask_gate(key, part):
    return column_mask(key, 11, DB, FB, 1)


def draw_mask_up(key, part):
    return column_mask(key, 23, DB, FB, 1)


def draw_mask_down(key, part):
    return column_mask(key, 37, FB, DB, 0)


def levels(stream_key, extent, pieces, low, high):
    def one(dim, parts):
        draws = jax.random.uniform(jax.random.fold_in(jax.random.fold_in(stream_key, 6), dim), (parts,), jnp.float32, low / len(pieces), high / len(pieces))
        return jnp.repeat(jnp.exp(draws), extent[dim] // parts).reshape((-1,) + (1,) * (len(extent) - dim - 1))

    level = one(*pieces[0])
    for cut in pieces[1:]:
        level = level * one(*cut)
    return level


def normal_values(rng, extent, spread, bound, pieces=(), held_as=jnp.bfloat16):
    factor_of = levels(rng, extent, pieces, -0.22, 0.18) if pieces else 1.0
    array = jax.random.normal(rng, extent, jnp.float32) * spread * factor_of
    return jnp.minimum(jnp.maximum(array, -bound), bound).astype(held_as)


def setup_inputs(seed: int = 0) -> dict:
    seeds = jax.random.split(jax.random.key(seed), 9)
    tokens = normal_values(seeds[0], (TOKENS, D), 1.0, 6.0, ((0, 32), (1, 4)))
    gate_weight = normal_values(seeds[1], (D, FF), D ** -0.5, 0.0625, ((0, 4), (1, 32)))
    up_weight = normal_values(seeds[2], (D, FF), D ** -0.5, 0.0625, ((0, 4), (1, 32)))
    down_weight = normal_values(seeds[3], (FF, D), FF ** -0.5, 0.03125, ((0, 32), (1, 4)))
    mask_gate = draw_mask_gate(jax.random.fold_in(seeds[8], 71), 0)
    mask_up = draw_mask_up(jax.random.fold_in(seeds[8], 71), 0)
    mask_down = draw_mask_down(jax.random.fold_in(seeds[8], 71), 0)
    cotangent = normal_values(seeds[7], (TOKENS, D), 0.25, 1.5, ((0, 32), (1, 4)))
    return dict(tokens=tokens, gate_weight=gate_weight, up_weight=up_weight, down_weight=down_weight, mask_gate=mask_gate, mask_up=mask_up, mask_down=mask_down, cotangent=cotangent)


def expand(mask):
    return jnp.repeat(jnp.repeat(mask, BLOCK, 0), BLOCK, 1).astype(jnp.bfloat16)


def reference(tokens, gate_weight, up_weight, down_weight, mask_gate, mask_up, mask_down, cotangent):
    keep_gate = expand(mask_gate)
    keep_up = expand(mask_up)
    keep_down = expand(mask_down)
    w_gate = gate_weight * keep_gate
    w_up = up_weight * keep_up
    w_down = down_weight * keep_down
    gate = jnp.dot(tokens, w_gate, preferred_element_type=jnp.float32)
    up = jnp.dot(tokens, w_up, preferred_element_type=jnp.float32)
    sigma = jax.nn.sigmoid(gate)
    hidden = (gate * sigma * up).astype(jnp.bfloat16)
    output = jnp.dot(hidden, w_down, preferred_element_type=jnp.float32).astype(jnp.bfloat16)
    dhid = lax.dot_general(cotangent, w_down, (((1,), (1,)), ((), ())), preferred_element_type=jnp.float32)
    dgate = (dhid * up * sigma * (1.0 + gate * (1.0 - sigma))).astype(jnp.bfloat16)
    dup = (dhid * gate * sigma).astype(jnp.bfloat16)
    grad_down = (lax.dot_general(hidden, cotangent, (((0,), (0,)), ((), ())), preferred_element_type=jnp.float32) * keep_down).astype(jnp.bfloat16)
    grad_gate = (lax.dot_general(tokens, dgate, (((0,), (0,)), ((), ())), preferred_element_type=jnp.float32) * keep_gate).astype(jnp.bfloat16)
    grad_up = (lax.dot_general(tokens, dup, (((0,), (0,)), ((), ())), preferred_element_type=jnp.float32) * keep_up).astype(jnp.bfloat16)
    first = lax.dot_general(dgate, w_gate, (((1,), (1,)), ((), ())), preferred_element_type=jnp.float32)
    second = lax.dot_general(dup, w_up, (((1,), (1,)), ((), ())), preferred_element_type=jnp.float32)
    grad_input = (first + second).astype(jnp.bfloat16)
    return output, grad_input, grad_gate, grad_up, grad_down
```

```python
import jax
import jax.numpy as jnp
from jax import lax
from jax.sharding import PartitionSpec as P

BLOCK = 64
NY, NZ, NX, NC = 4, 4, 4, 2
F32, BF16 = jnp.float32, jnp.bfloat16


def index(y, z, x, c):
    return ((y * NZ + z % NZ) * NX + x % NX) * NC + c % NC


def fetch(value, source):
    pairs = []
    for y in range(NY):
        for z in range(NZ):
            for x in range(NX):
                for c in range(NC):
                    sy, sz, sx, sc = source(y, z, x, c)
                    pairs.append((index(sy % NY, sz, sx, sc), index(y, z, x, c)))
    return lax.ppermute(value, ("row", "col"), pairs)


def from_x(value, d):
    return fetch(value, lambda y, z, x, c: (y, z, x + d, c))


def from_slot(value, k):
    return fetch(value, lambda y, z, x, c: (y, z + y + k, x, c))


def to_slot(value, k):
    return fetch(value, lambda y, z, x, c: (y, z - y - k, x, c))


def from_y(value, d):
    return fetch(value, lambda y, z, x, c: (y + d, z, x, c))


def swap(value):
    return fetch(value, lambda y, z, x, c: (y, z, x, c + 1))


def expand_rows(cols, rows):
    return jnp.broadcast_to(cols[:, None, :], (cols.shape[0], BLOCK, cols.shape[1])).reshape(rows, cols.shape[1])


def mask_cols(mask):
    n = mask.shape[1]
    spread = (jnp.arange(n)[:, None] == (jnp.arange(n * BLOCK) // BLOCK)[None, :]).astype(BF16)
    return jnp.dot(mask.astype(BF16), spread, preferred_element_type=F32).astype(BF16)


def dot_nn(a, b):
    return jnp.dot(a, b, preferred_element_type=F32)


def dot_nt(a, b):
    return lax.dot_general(a, b, (((1,), (1,)), ((), ())), preferred_element_type=F32)


def dot_tn(a, b):
    return lax.dot_general(a, b, (((0,), (0,)), ((), ())), preferred_element_type=F32)


def gather_zx(a):
    first = jnp.stack([from_slot(a, k) for k in range(NZ)])
    return jnp.stack([first] + [from_x(first, d) for d in range(1, NX)], axis=1)


def gather_xz(a):
    first = jnp.stack([a] + [from_x(a, d) for d in range(1, NX)])
    return jnp.stack([from_slot(first, k) for k in range(NZ)])


def row_scatter(p0, p1):
    b0, b1 = p0.astype(BF16), p1.astype(BF16)
    r0 = from_y(b0[2], -1)
    r1 = from_y(b1[2], 1)
    direct0 = from_y(b0[3], 1)
    direct1 = from_y(b1[1], -1)
    relay0 = from_y((p0[1] + r0.astype(F32)).astype(BF16), -1)
    relay1 = from_y((p1[3] + r1.astype(F32)).astype(BF16), 1)
    s0 = p0[0] + direct0.astype(F32) + relay0.astype(F32)
    s1 = p1[0] + direct1.astype(F32) + relay1.astype(F32)
    return s0, s1


def row_gather(own):
    plus = from_y(own, 1)
    minus = from_y(own, -1)
    far0 = from_y(minus[0], -1)
    far1 = from_y(plus[1], 1)
    h0 = jnp.stack([own[0], plus[0], far0, minus[0]])
    h1 = jnp.stack([own[1], plus[1], far1, minus[1]])
    return h0, h1


def combine_core(p0, p1):
    s = p0 + swap(p1.astype(BF16)).astype(F32)
    return s.reshape(NZ, NX, -1, s.shape[-1])


def scatter_xz(s):
    t = s[:, 0]
    for d in range(1, NX):
        t = t + from_x(s[:, d].astype(BF16), -d).astype(F32)
    u = jnp.zeros_like(t[0])
    for k in range(NZ):
        u = u + to_slot(t[k].astype(BF16), k).astype(F32)
    return u.astype(BF16)


def scatter_zx(s):
    t = jnp.zeros_like(s[0])
    for k in range(NZ):
        t = t + to_slot(s[k].astype(BF16), k).astype(F32)
    u = t[0]
    for d in range(1, NX):
        u = u + from_x(t[d].astype(BF16), -d).astype(F32)
    return u.astype(BF16)


def body(tokens, gate_weight, up_weight, down_weight, mask_gate, mask_up, mask_down, cotangent):
    rows, width = gate_weight.shape
    kg, ku, kd = mask_cols(mask_gate), mask_cols(mask_up), mask_cols(mask_down)
    keep_gate, keep_up = expand_rows(kg, rows), expand_rows(ku, rows)
    keep_down = expand_rows(kd, width)
    w_gate = gate_weight * keep_gate
    w_up = up_weight * keep_up
    w_down = down_weight * keep_down

    x0 = gather_zx(tokens).reshape(-1, rows)
    c0 = gather_xz(cotangent).reshape(-1, rows)
    x1 = swap(x0)
    c1 = swap(c0)
    half = x0.shape[0]
    part = half // NY

    def chunks(p):
        return p.reshape(NY, part, p.shape[1])

    both = jnp.concatenate([w_gate, w_up], axis=1)
    gu0, gu1 = row_scatter(chunks(dot_nn(x0, both)), chunks(dot_nn(x1, both)))
    dh0, dh1 = row_scatter(chunks(dot_nt(c0, w_down)), chunks(dot_nt(c1, w_down)))
    gu = jnp.stack([gu0, gu1])
    dhid = jnp.stack([dh0, dh1])
    gate, up = gu[..., :width], gu[..., width:]
    sigma = jax.nn.sigmoid(gate)
    hidden = (gate * sigma * up).astype(BF16)
    dgate = (dhid * up * sigma * (1.0 + gate * (1.0 - sigma))).astype(BF16)
    dup = (dhid * gate * sigma).astype(BF16)

    h0, h1 = (h.reshape(half, width) for h in row_gather(hidden))
    o = combine_core(dot_nn(h0, w_down), dot_nn(h1, w_down))
    output = scatter_xz(o)
    d0, d1 = (d.reshape(half, 2 * width) for d in row_gather(jnp.concatenate([dgate, dup], axis=-1)))
    i = combine_core(dot_nt(d0, both), dot_nt(d1, both))
    grad_input = scatter_zx(i)

    grad_down = ((dot_tn(h0, c0) + dot_tn(h1, c1)) * keep_down).astype(BF16)
    dg = dot_tn(x0, d0[:, :width]) + dot_tn(x1, d1[:, :width])
    du = dot_tn(x0, d0[:, width:]) + dot_tn(x1, d1[:, width:])
    grad_gate = (dg * keep_gate).astype(BF16)
    grad_up = (du * keep_up).astype(BF16)
    return (output, grad_input, grad_gate, grad_up, grad_down)


def solution(mesh):
    act, weight = P("col", "row"), P("row", "col")
    return jax.shard_map(
        body,
        mesh=mesh,
        in_specs=(act, weight, weight, act, weight, weight, act, act),
        out_specs=(act, act, weight, weight, act),
        check_vma=False,
    )
```

```python
import jax
import jax.numpy as jnp
from jax import lax
from jax.sharding import Mesh, PartitionSpec as P

BLOCK = 64
NY, NZ, NX, NC = 4, 4, 4, 2
F32, BF16 = jnp.float32, jnp.bfloat16


def index(y, z, x, c):
    return ((y * NZ + z % NZ) * NX + x % NX) * NC + c % NC


def fetch(value, source):
    pairs = []
    for y in range(NY):
        for z in range(NZ):
            for x in range(NX):
                for c in range(NC):
                    sy, sz, sx, sc = source(y, z, x, c)
                    pairs.append((index(sy % NY, sz, sx, sc), index(y, z, x, c)))
    return lax.ppermute(value, ("y", "z", "x", "c"), pairs)


def from_x(value, d):
    return fetch(value, lambda y, z, x, c: (y, z, x + d, c))


def from_z(value, d):
    return fetch(value, lambda y, z, x, c: (y, z + d, x, c))


def unroll_z(value):
    return fetch(value, lambda y, z, x, c: (y, z - y, x, c))


def from_y(value, d):
    return fetch(value, lambda y, z, x, c: (y + d, z, x, c))


def swap(value):
    return fetch(value, lambda y, z, x, c: (y, z, x, c + 1))


def expand_rows(cols, rows):
    return jnp.broadcast_to(cols[:, None, :], (cols.shape[0], BLOCK, cols.shape[1])).reshape(rows, cols.shape[1])


def mask_cols(mask):
    n = mask.shape[1]
    spread = (jnp.arange(n)[:, None] == (jnp.arange(n * BLOCK) // BLOCK)[None, :]).astype(BF16)
    return jnp.dot(mask.astype(BF16), spread, preferred_element_type=F32).astype(BF16)


def dot_nn(a, b):
    return jnp.dot(a, b, preferred_element_type=F32)


def dot_nt(a, b):
    return lax.dot_general(a, b, (((1,), (1,)), ((), ())), preferred_element_type=F32)


def dot_tn(a, b):
    return lax.dot_general(a, b, (((0,), (0,)), ((), ())), preferred_element_type=F32)


def gather_xz(a):
    t = lax.all_gather(lax.all_gather(a, "x", axis=0, tiled=True), "z", axis=0, tiled=True)
    n = t.shape[0]
    return lax.dynamic_slice_in_dim(jnp.concatenate([t, t]), lax.axis_index("y") * (n // NY), n, 0)


def row_scatter(p0, p1):
    b0, b1 = p0.astype(BF16), p1.astype(BF16)
    r0 = from_y(b0[2], -1)
    r1 = from_y(b1[2], 1)
    direct0 = from_y(b0[3], 1)
    direct1 = from_y(b1[1], -1)
    relay0 = from_y((p0[1] + r0.astype(F32)).astype(BF16), -1)
    relay1 = from_y((p1[3] + r1.astype(F32)).astype(BF16), 1)
    s0 = p0[0] + direct0.astype(F32) + relay0.astype(F32)
    s1 = p1[0] + direct1.astype(F32) + relay1.astype(F32)
    return s0, s1


def row_gather(own):
    plus = from_y(own, 1)
    minus = from_y(own, -1)
    far0 = from_y(minus[0], -1)
    far1 = from_y(plus[1], 1)
    h0 = jnp.stack([own[0], plus[0], far0, minus[0]])
    h1 = jnp.stack([own[1], plus[1], far1, minus[1]])
    return h0, h1


def combine_core(p0, p1):
    return p0 + swap(p1.astype(BF16)).astype(F32)


def scatter_offload(s):
    t = lax.psum_scatter(s, "z", scatter_dimension=0, tiled=True)
    u = lax.psum_scatter(t, "x", scatter_dimension=0, tiled=True)
    return unroll_z(u.astype(BF16))


def scatter_xz(s):
    s = s.reshape(NZ, NX, -1, s.shape[-1])
    y, z, x = lax.axis_index("y"), lax.axis_index("z"), lax.axis_index("x")
    t = lax.dynamic_index_in_dim(s, x, 1, False)
    for d in (1, 3, 2):
        t = t + from_x(lax.dynamic_index_in_dim(s, (x + d) % NX, 1, False).astype(BF16), -d).astype(F32)
    u = lax.dynamic_index_in_dim(t, (z - y) % NZ, 0, False)
    for d in (1, 3, 2):
        u = u + from_z(lax.dynamic_index_in_dim(t, (z + d - y) % NZ, 0, False).astype(BF16), -d).astype(F32)
    return u.astype(BF16)


def body(tokens, gate_weight, up_weight, down_weight, mask_gate, mask_up, mask_down, cotangent):
    rows, width = gate_weight.shape
    kg, ku, kd = mask_cols(mask_gate), mask_cols(mask_up), mask_cols(mask_down)
    keep_gate, keep_up = expand_rows(kg, rows), expand_rows(ku, rows)
    keep_down = expand_rows(kd, width)
    w_gate = gate_weight * keep_gate
    w_up = up_weight * keep_up
    w_down = down_weight * keep_down

    x0 = gather_xz(tokens)
    x0, cotangent = lax.optimization_barrier((x0, cotangent))
    c0 = gather_xz(cotangent)
    x1 = swap(x0)
    c1 = swap(c0)
    half = x0.shape[0]
    part = half // NY

    def chunks(p):
        return p.reshape(NY, part, p.shape[1])

    both = jnp.concatenate([w_gate, w_up], axis=1)
    gu0, gu1 = row_scatter(chunks(dot_nn(x0, both)), chunks(dot_nn(x1, both)))
    dh0, dh1 = row_scatter(chunks(dot_nt(c0, w_down)), chunks(dot_nt(c1, w_down)))
    gu = jnp.stack([gu0, gu1])
    dhid = jnp.stack([dh0, dh1])
    gate, up = gu[..., :width], gu[..., width:]
    sigma = jax.nn.sigmoid(gate)
    hidden = (gate * sigma * up).astype(BF16)
    dgate = (dhid * up * sigma * (1.0 + gate * (1.0 - sigma))).astype(BF16)
    dup = (dhid * gate * sigma).astype(BF16)

    h0, h1 = (h.reshape(half, width) for h in row_gather(hidden))
    o = combine_core(dot_nn(h0, w_down), dot_nn(h1, w_down))
    output = scatter_offload(o)
    d0, d1 = (d.reshape(half, 2 * width) for d in row_gather(jnp.concatenate([dgate, dup], axis=-1)))
    i = combine_core(dot_nt(d0, both), dot_nt(d1, both))
    x0, x1, i = lax.optimization_barrier((x0, x1, i))
    grad_input = scatter_xz(i)

    grad_down = ((dot_tn(h0, c0) + dot_tn(h1, c1)) * keep_down).astype(BF16)
    dg = dot_tn(x0, d0[:, :width]) + dot_tn(x1, d1[:, :width])
    du = dot_tn(x0, d0[:, width:]) + dot_tn(x1, d1[:, width:])
    grad_gate = (dg * keep_gate).astype(BF16)
    grad_up = (du * keep_up).astype(BF16)
    return (output, grad_input, grad_gate, grad_up, grad_down)


def solution(mesh):
    grid = Mesh(mesh.devices.reshape(NY, NZ, NX, NC), ("y", "z", "x", "c"))
    act, weight = P(("z", "x", "c"), "y"), P("y", ("z", "x", "c"))
    return jax.shard_map(
        body,
        mesh=grid,
        in_specs=(act, weight, weight, act, weight, weight, act, act),
        out_specs=(act, act, weight, weight, act),
        check_vma=False,
    )
```

```python
import jax
import jax.numpy as jnp
from jax import lax
from jax.sharding import PartitionSpec as P

BLOCK = 64
NY, NZ, NX, NC = 4, 4, 4, 2
F32, BF16 = jnp.float32, jnp.bfloat16


def index(y, z, x, c):
    return ((y * NZ + z % NZ) * NX + x % NX) * NC + c % NC


def fetch(value, source):
    pairs = []
    for y in range(NY):
        for z in range(NZ):
            for x in range(NX):
                for c in range(NC):
                    sy, sz, sx, sc = source(y, z, x, c)
                    pairs.append((index(sy % NY, sz, sx, sc), index(y, z, x, c)))
    return lax.ppermute(value, ("row", "col"), pairs)


def from_x(value, d):
    return fetch(value, lambda y, z, x, c: (y, z, x + d, c))


def from_slot(value, k):
    return fetch(value, lambda y, z, x, c: (y, z + y + k, x, c))


def to_slot(value, k):
    return fetch(value, lambda y, z, x, c: (y, z - y - k, x, c))


def from_y(value, d):
    return fetch(value, lambda y, z, x, c: (y + d, z, x, c))


def swap(value):
    return fetch(value, lambda y, z, x, c: (y, z, x, c + 1))


def expand_rows(cols, rows):
    return jnp.broadcast_to(cols[:, None, :], (cols.shape[0], BLOCK, cols.shape[1])).reshape(rows, cols.shape[1])


def mask_cols(mask):
    n = mask.shape[1]
    spread = (jnp.arange(n)[:, None] == (jnp.arange(n * BLOCK) // BLOCK)[None, :]).astype(BF16)
    return jnp.dot(mask.astype(BF16), spread, preferred_element_type=F32).astype(BF16)


def dot_nn(a, b):
    return jnp.dot(a, b, preferred_element_type=F32)


def dot_nt(a, b):
    return lax.dot_general(a, b, (((1,), (1,)), ((), ())), preferred_element_type=F32)


def dot_tn(a, b):
    return lax.dot_general(a, b, (((0,), (0,)), ((), ())), preferred_element_type=F32)


def gather_x(a):
    return jnp.stack([a] + [from_x(a, d) for d in range(1, NX)])


def gather_slots(a):
    return jnp.stack([from_slot(a, k) for k in range(NZ)])


def gather_pair(tokens, cotangent):
    first = gather_slots(tokens)
    other = gather_x(cotangent)
    x0 = jnp.stack([first] + [from_x(first, d) for d in range(1, NX)], axis=1)
    x0, other = lax.optimization_barrier((x0, other))
    return x0, gather_slots(other)


def row_scatter(p0, p1):
    b0, b1 = p0.astype(BF16), p1.astype(BF16)
    r0 = from_y(b0[2], -1)
    r1 = from_y(b1[2], 1)
    direct0 = from_y(b0[3], 1)
    direct1 = from_y(b1[1], -1)
    relay0 = from_y((p0[1] + r0.astype(F32)).astype(BF16), -1)
    relay1 = from_y((p1[3] + r1.astype(F32)).astype(BF16), 1)
    s0 = p0[0] + direct0.astype(F32) + relay0.astype(F32)
    s1 = p1[0] + direct1.astype(F32) + relay1.astype(F32)
    return s0, s1


def row_gather(own):
    plus = from_y(own, 1)
    minus = from_y(own, -1)
    far0 = from_y(minus[0], -1)
    far1 = from_y(plus[1], 1)
    h0 = jnp.stack([own[0], plus[0], far0, minus[0]])
    h1 = jnp.stack([own[1], plus[1], far1, minus[1]])
    return h0, h1


def combine_core(p0, p1):
    s = p0 + swap(p1.astype(BF16)).astype(F32)
    return s.reshape(NZ, NX, -1, s.shape[-1])


def scatter_x(s):
    t = s[:, 0]
    for d in (1, 3, 2):
        t = t + from_x(s[:, d].astype(BF16), -d).astype(F32)
    return t


def scatter_slots(t):
    u = jnp.zeros_like(t[0])
    for k in range(NZ):
        u = u + to_slot(t[k].astype(BF16), k).astype(F32)
    return u.astype(BF16)


def body(tokens, gate_weight, up_weight, down_weight, mask_gate, mask_up, mask_down, cotangent):
    rows, width = gate_weight.shape
    kg, ku, kd = mask_cols(mask_gate), mask_cols(mask_up), mask_cols(mask_down)
    keep_gate, keep_up = expand_rows(kg, rows), expand_rows(ku, rows)
    keep_down = expand_rows(kd, width)
    w_gate = gate_weight * keep_gate
    w_up = up_weight * keep_up
    w_down = down_weight * keep_down

    x0, c0 = (a.reshape(-1, rows) for a in gather_pair(tokens, cotangent))
    x1 = swap(x0)
    c1 = swap(c0)
    half = x0.shape[0]
    part = half // NY

    def chunks(p):
        return p.reshape(NY, part, p.shape[1])

    both = jnp.concatenate([w_gate, w_up], axis=1)
    gu0, gu1 = row_scatter(chunks(dot_nn(x0, both)), chunks(dot_nn(x1, both)))
    dh0, dh1 = row_scatter(chunks(dot_nt(c0, w_down)), chunks(dot_nt(c1, w_down)))
    gu = jnp.stack([gu0, gu1])
    dhid = jnp.stack([dh0, dh1])
    gate, up = gu[..., :width], gu[..., width:]
    sigma = jax.nn.sigmoid(gate)
    hidden = (gate * sigma * up).astype(BF16)
    dgate = (dhid * up * sigma * (1.0 + gate * (1.0 - sigma))).astype(BF16)
    dup = (dhid * gate * sigma).astype(BF16)

    h0, h1 = (h.reshape(half, width) for h in row_gather(hidden))
    o = combine_core(dot_nn(h0, w_down), dot_nn(h1, w_down))
    o = scatter_x(o)
    grad_down = ((dot_tn(h0, c0) + dot_tn(h1, c1)) * keep_down).astype(BF16)
    d0, d1 = (d.reshape(half, 2 * width) for d in row_gather(jnp.concatenate([dgate, dup], axis=-1)))
    d0, d1, o, grad_down = lax.optimization_barrier((d0, d1, o, grad_down))
    output = scatter_slots(o)
    i = combine_core(dot_nt(d0, both), dot_nt(d1, both))
    x0, x1, d0, d1, i = lax.optimization_barrier((x0, x1, d0, d1, i))
    i = scatter_x(i)
    dg = dot_tn(x0, d0[:, :width]) + dot_tn(x1, d1[:, :width])
    du = dot_tn(x0, d0[:, width:]) + dot_tn(x1, d1[:, width:])
    grad_gate = (dg * keep_gate).astype(BF16)
    grad_up = (du * keep_up).astype(BF16)
    i, grad_gate, grad_up = lax.optimization_barrier((i, grad_gate, grad_up))
    grad_input = scatter_slots(i)
    return (output, grad_input, grad_gate, grad_up, grad_down)


def solution(mesh):
    act, weight = P("col", "row"), P("row", "col")
    return jax.shard_map(
        body,
        mesh=mesh,
        in_specs=(act, weight, weight, act, weight, weight, act, act),
        out_specs=(act, act, weight, weight, act),
        check_vma=False,
    )
```

```python
import jax
import jax.numpy as jnp
from jax import lax
from jax.sharding import PartitionSpec as P

BLOCK = 64
NY, NZ, NX, NC = 4, 4, 4, 2
F32, BF16 = jnp.float32, jnp.bfloat16


def index(y, z, x, c):
    return ((y * NZ + z % NZ) * NX + x % NX) * NC + c % NC


def fetch(value, source):
    pairs = []
    for y in range(NY):
        for z in range(NZ):
            for x in range(NX):
                for c in range(NC):
                    sy, sz, sx, sc = source(y, z, x, c)
                    pairs.append((index(sy % NY, sz, sx, sc), index(y, z, x, c)))
    return lax.ppermute(value, ("row", "col"), pairs)


def from_x(value, d):
    return fetch(value, lambda y, z, x, c: (y, z, x + d, c))


def from_slot(value, k):
    return fetch(value, lambda y, z, x, c: (y, z + y + k, x, c))


def to_slot(value, k):
    return fetch(value, lambda y, z, x, c: (y, z - y - k, x, c))


def from_y(value, d):
    return fetch(value, lambda y, z, x, c: (y + d, z, x, c))


def swap(value):
    return fetch(value, lambda y, z, x, c: (y, z, x, c + 1))


def expand_rows(cols, rows):
    return jnp.broadcast_to(cols[:, None, :], (cols.shape[0], BLOCK, cols.shape[1])).reshape(rows, cols.shape[1])


def mask_cols(mask):
    n = mask.shape[1]
    spread = (jnp.arange(n)[:, None] == (jnp.arange(n * BLOCK) // BLOCK)[None, :]).astype(BF16)
    return jnp.dot(mask.astype(BF16), spread, preferred_element_type=F32).astype(BF16)


def dot_nn(a, b):
    return jnp.dot(a, b, preferred_element_type=F32)


def dot_nt(a, b):
    return lax.dot_general(a, b, (((1,), (1,)), ((), ())), preferred_element_type=F32)


def dot_tn(a, b):
    return lax.dot_general(a, b, (((0,), (0,)), ((), ())), preferred_element_type=F32)


def gather_zx(a):
    first = jnp.stack([from_slot(a, k) for k in range(NZ)])
    return jnp.stack([first] + [from_x(first, d) for d in range(1, NX)], axis=1)


def gather_xz(a):
    first = jnp.stack([a] + [from_x(a, d) for d in range(1, NX)])
    return jnp.stack([from_slot(first, k) for k in range(NZ)])


def row_scatter(p0, p1):
    b0, b1 = p0.astype(BF16), p1.astype(BF16)
    r0 = from_y(b0[2], -1)
    r1 = from_y(b1[2], 1)
    direct0 = from_y(b0[3], 1)
    direct1 = from_y(b1[1], -1)
    relay0 = from_y((p0[1] + r0.astype(F32)).astype(BF16), -1)
    relay1 = from_y((p1[3] + r1.astype(F32)).astype(BF16), 1)
    s0 = p0[0] + direct0.astype(F32) + relay0.astype(F32)
    s1 = p1[0] + direct1.astype(F32) + relay1.astype(F32)
    return s0, s1


def row_gather(own):
    plus = from_y(own, 1)
    minus = from_y(own, -1)
    far0 = from_y(minus[0], -1)
    far1 = from_y(plus[1], 1)
    far0, far1 = lax.optimization_barrier((far0, far1))
    h0 = jnp.stack([own[0], plus[0], far0, minus[0]])
    h1 = jnp.stack([own[1], plus[1], far1, minus[1]])
    return h0, h1


def combine_core(p0, p1):
    got = swap(jnp.stack([p.astype(BF16) for p in p1])).astype(F32)
    return [(p + g).reshape(NZ, NX, -1, p.shape[-1]) for p, g in zip(p0, got)]


def scatter_x(s):
    t = [a[:, 0] for a in s]
    for d in range(1, NX):
        got = from_x(jnp.stack([a[:, d].astype(BF16) for a in s]), -d).astype(F32)
        t = [a + g for a, g in zip(t, got)]
    return t


def scatter_slots(t):
    u = [jnp.zeros_like(a[0]) for a in t]
    for k in range(NZ):
        got = to_slot(jnp.stack([a[k].astype(BF16) for a in t]), k).astype(F32)
        u = [a + g for a, g in zip(u, got)]
    return [a.astype(BF16) for a in u]


def body(tokens, gate_weight, up_weight, down_weight, mask_gate, mask_up, mask_down, cotangent):
    rows, width = gate_weight.shape
    kg, ku, kd = mask_cols(mask_gate), mask_cols(mask_up), mask_cols(mask_down)
    keep_gate, keep_up = expand_rows(kg, rows), expand_rows(ku, rows)
    keep_down = expand_rows(kd, width)
    w_gate = gate_weight * keep_gate
    w_up = up_weight * keep_up
    w_down = down_weight * keep_down

    x0 = gather_zx(tokens).reshape(-1, rows)
    c0 = gather_xz(cotangent).reshape(-1, rows)
    x1 = swap(x0)
    c1 = swap(c0)
    half = x0.shape[0]
    part = half // NY

    def chunks(p):
        return p.reshape(NY, part, p.shape[1])

    both = jnp.concatenate([w_gate, w_up], axis=1)
    gu0, gu1 = row_scatter(chunks(dot_nn(x0, both)), chunks(dot_nn(x1, both)))
    dh0, dh1 = row_scatter(chunks(dot_nt(c0, w_down)), chunks(dot_nt(c1, w_down)))
    gu = jnp.stack([gu0, gu1])
    dhid = jnp.stack([dh0, dh1])
    gate, up = gu[..., :width], gu[..., width:]
    sigma = jax.nn.sigmoid(gate)
    hidden = (gate * sigma * up).astype(BF16)
    dgate = (dhid * up * sigma * (1.0 + gate * (1.0 - sigma))).astype(BF16)
    dup = (dhid * gate * sigma).astype(BF16)

    a0, a1 = (a.reshape(half, 3 * width) for a in row_gather(jnp.concatenate([hidden, dgate, dup], axis=-1)))
    h0, d0 = a0[:, :width], a0[:, width:]
    h1, d1 = a1[:, :width], a1[:, width:]
    s = combine_core([dot_nn(h0, w_down), dot_nt(d0, both)], [dot_nn(h1, w_down), dot_nt(d1, both)])
    s, x0, x1, c0, c1 = lax.optimization_barrier((s, x0, x1, c0, c1))
    t = scatter_x(s)
    grad_down = ((dot_tn(h0, c0) + dot_tn(h1, c1)) * keep_down).astype(BF16)
    dg = dot_tn(x0, d0[:, :width]) + dot_tn(x1, d1[:, :width])
    du = dot_tn(x0, d0[:, width:]) + dot_tn(x1, d1[:, width:])
    grad_gate = (dg * keep_gate).astype(BF16)
    grad_up = (du * keep_up).astype(BF16)
    t, grad_down, grad_gate, grad_up = lax.optimization_barrier((t, grad_down, grad_gate, grad_up))
    output, grad_input = scatter_slots(t)
    return (output, grad_input, grad_gate, grad_up, grad_down)


def solution(mesh):
    act, weight = P("col", "row"), P("row", "col")
    return jax.shard_map(
        body,
        mesh=mesh,
        in_specs=(act, weight, weight, act, weight, weight, act, act),
        out_specs=(act, act, weight, weight, act),
        check_vma=False,
    )
```
